128 devices in a mesh: gx: 8 (over y, core), gy: 16 (over z, x).
Axes of the slice: x: 4, y: 4, z: 4, core: 2. Of those that a mesh axis runs over, the one named last changes fastest.
Arguments:
- displacement: float32 [3, 192, 128, 128], P(None, 'gx', 'gy'), may hold values from -6 to 6
- velocity: float32 [3, 192, 128, 128], P(None, 'gx', 'gy'), may hold values from -6 to 6
- external_force: float32 [3, 192, 128, 128], P(None, 'gx', 'gy'), may hold values from -6 to 6
- node_mass: float32 [192, 128, 128], P('gx', 'gy'), may hold values from 0.5 to 2
- stiffness: float32 [192, 128, 128], P('gx', 'gy'), may hold values from 0.5 to 2
- cloak_list: int32 [8, 16, 48], P('gx'), may hold values from -1 to 191, as said below
- micro_state: float32 [8, 16, 128, 48, 128], P('gx', 'gy'), may hold values from -6 to 6
- localization: float32 [256, 6], replicated, may hold values from -3.6 to 3.6
- modes: float32 [256, 128], replicated, may hold values from -0.5 to 0.5
- point_weight: float32 [256], replicated, may hold values from 0.5 to 2
- point_modulus: float32 [256], replicated, may hold values from 1 to 10
- softening: float32 [256], replicated, may hold values from 0.2 to 2
Outputs:
- displacement_next: float32 [3, 192, 128, 128], P(None, 'gx', 'gy')
- velocity_next: float32 [3, 192, 128, 128], P(None, 'gx', 'gy')
- micro_state_next: float32 [8, 16, 128, 48, 128], P('gx', 'gy')
The draws below stay inside these ranges and needn't reach their ends.
Inputs may be any that keep to these rules, and one draw needn't show every extreme that they name: cloak_list[p, t, :] holds distinct pencil indices x * 8 + y of tile (p, t) in ascending order followed by -1; in every gx index exactly one tile lists 48 pencils and every other tile lists between 22 and 24 pencils, 22 reached in every gx index; the tiles sharing a gx index list exactly 384 pencils together.
All inputs are finite; a program needn't handle non-finite values.
Results may differ from the reference program's by a relative error of at most 0.0003.
Values sent between devices are 32-bit elements; how exact they have to be, the bound alone decides.
A program may use at most 64 MiB of HBM per device.

```python
import math
import jax
import jax.numpy as jnp
from jax import lax

CX = 24
CY = 8
LZ = 128
P_SIZE = 256
M = 128
ITERS = 3
NX = 192
NY = 128
OWN = 24
CMAX = 48
N_GX = 8
N_GY = 16


def tile_list(subkey, listed_count):
    shuffled = jax.random.permutation(subkey, CX * CY)
    marked = jnp.where(jnp.arange(CX * CY) < listed_count, shuffled, CX * CY)
    ranked = jnp.sort(marked)[:CMAX]
    return jnp.where(ranked >= CX * CY, -1, ranked).astype(jnp.int32)


def row_lists(subkey):
    busiest = jax.random.randint(jax.random.fold_in(subkey, 1), (), 0, N_GY)
    others_count = N_GY - 1
    base_short = OWN // others_count
    extra_short = OWN % others_count
    order = jax.random.permutation(jax.random.fold_in(subkey, 2), others_count)
    shortfall = base_short + (order < extra_short).astype(jnp.int32)
    others = OWN - shortfall
    column = jnp.arange(N_GY)
    shifted = jnp.minimum(jnp.where(column > busiest, column - 1, column), N_GY - 2)
    tile_counts = jnp.where(column == busiest, CMAX, others[shifted])
    tile_keys = jax.vmap(jax.random.fold_in, in_axes=(None, 0))(subkey, column + 100)
    return jax.vmap(tile_list)(tile_keys, tile_counts)


def draw_cloak_list(key, part):
    row_index = jnp.arange(N_GX)
    row_keys = jax.vmap(jax.random.fold_in, in_axes=(None, 0))(key, row_index * 1000 + 7)
    return jax.vmap(row_lists)(row_keys)


def levels(rng, extent, pieces, low, high):
    def one(dim, parts):
        draws = jax.random.uniform(jax.random.fold_in(jax.random.fold_in(rng, 6), dim), (parts,), jnp.float32, low / len(pieces), high / len(pieces))
        return jnp.repeat(jnp.exp(draws), extent[dim] // parts).reshape((-1,) + (1,) * (len(extent) - dim - 1))

    factor_of = one(*pieces[0])
    for cut in pieces[1:]:
        factor_of = factor_of * one(*cut)
    return factor_of


def noise(rng, extent, width, reach, split=(), held_as=jnp.bfloat16):
    loudness = levels(rng, extent, split, -0.22, 0.18) if split else 1.0
    result = jax.random.normal(rng, extent, jnp.float32) * width * loudness
    return jnp.minimum(jnp.maximum(result, -reach), reach).astype(held_as)


def setup_inputs(seed: int = 0) -> dict:
    splits = jax.random.split(jax.random.key(seed), 13)
    displacement = noise(splits[0], (3, NX, NY, LZ), 1.0, 6.0, ((1, 8), (2, 16)), jnp.float32)
    velocity = noise(splits[1], (3, NX, NY, LZ), 1.0, 6.0, ((1, 8), (2, 16)), jnp.float32)
    external_force = noise(splits[2], (3, NX, NY, LZ), 1.0, 6.0, ((1, 8), (2, 16)), jnp.float32)
    node_mass = jnp.clip(jnp.exp(math.log(2.0) - 1.3862944 * jax.random.uniform(splits[3], (NX, NY, LZ), jnp.float32) ** levels(splits[3], (NX, NY, LZ), ((0, 8), (1, 16)), -0.2, 0.2)), 0.5, 2.0)
    stiffness = jnp.clip(jnp.exp(math.log(2.0) - 1.3862944 * jax.random.uniform(splits[4], (NX, NY, LZ), jnp.float32) ** levels(splits[4], (NX, NY, LZ), ((0, 8), (1, 16)), -0.2, 0.2)), 0.5, 2.0)
    cloak_list = draw_cloak_list(jax.random.fold_in(splits[12], 71), 0)
    micro_state = noise(splits[6], (N_GX, N_GY, M, CMAX, LZ), 1.0, 6.0, ((0, 8), (1, 16)), jnp.float32)
    localization = noise(splits[7], (P_SIZE, 6), 0.6, 3.6, (), jnp.float32)
    modes = noise(splits[8], (P_SIZE, M), M ** -0.5, 0.5, (), jnp.float32)
    point_weight = jnp.clip(jnp.exp(jax.random.uniform(splits[9], (P_SIZE,), jnp.float32, math.log(0.5), math.log(2.0))), 0.5, 2.0)
    point_modulus = jnp.clip(jnp.exp(jax.random.uniform(splits[10], (P_SIZE,), jnp.float32, math.log(1.0), math.log(10.0))), 1.0, 10.0)
    softening = jnp.clip(jnp.exp(jax.random.uniform(splits[11], (P_SIZE,), jnp.float32, math.log(0.2), math.log(2.0))), 0.2, 2.0)
    return dict(displacement=displacement, velocity=velocity, external_force=external_force, node_mass=node_mass, stiffness=stiffness, cloak_list=cloak_list, micro_state=micro_state, localization=localization, modes=modes, point_weight=point_weight, point_modulus=point_modulus, softening=softening)


step_size = 0.25
highest = lax.Precision.HIGHEST

def pair_mean(values_in, dimension):
    upper = lax.slice_in_dim(values_in, 1, values_in.shape[dimension], axis=dimension)
    lower = lax.slice_in_dim(values_in, 0, values_in.shape[dimension] - 1, axis=dimension)
    return 0.5 * (upper + lower)

def pair_diff(values_in, dimension):
    upper = lax.slice_in_dim(values_in, 1, values_in.shape[dimension], axis=dimension)
    lower = lax.slice_in_dim(values_in, 0, values_in.shape[dimension] - 1, axis=dimension)
    return upper - lower

def voigt_strain(node_field):
    first_slope = pair_mean(pair_mean(pair_diff(node_field, 1), 2), 3)
    second_slope = pair_mean(pair_mean(pair_diff(node_field, 2), 1), 3)
    third_slope = pair_mean(pair_mean(pair_diff(node_field, 3), 1), 2)
    return jnp.stack([first_slope[0], second_slope[1], third_slope[2], third_slope[1] + second_slope[2], third_slope[0] + first_slope[2], second_slope[0] + first_slope[1]])

def linear_stress(strain, stiffness):
    volume_strain = strain[0] + strain[1] + strain[2]
    normal = [stiffness * (volume_strain + 2.0 * strain[column]) for column in range(3)]
    shears = [stiffness * strain[column] for column in range(3, 6)]
    return jnp.stack(normal + shears)

def assemble(stress, low_pad, high_pad):
    widths = ((0, 0), (low_pad, high_pad), (low_pad, high_pad), (1, 0))
    first_flux = jnp.pad(jnp.stack([stress[0], stress[5], stress[4]]), widths)
    second_flux = jnp.pad(jnp.stack([stress[5], stress[1], stress[3]]), widths)
    third_flux = jnp.pad(jnp.stack([stress[4], stress[3], stress[2]]), widths)
    return -(pair_diff(pair_mean(pair_mean(first_flux, 2), 3), 1) + pair_diff(pair_mean(pair_mean(second_flux, 1), 3), 2) + pair_diff(pair_mean(pair_mean(third_flux, 1), 2), 3))

def tangent_inverse(modes, point_weight, point_modulus):
    weights = point_weight * point_modulus / modes.shape[0]
    matrix = jnp.dot(modes.T * weights[None, :], modes, precision=highest)
    factor = jnp.linalg.cholesky(matrix)
    identity = jnp.eye(modes.shape[1], dtype=matrix.dtype)
    return jax.scipy.linalg.cho_solve((factor, True), identity)

def respond(point_strain, point_modulus, softening):
    return point_modulus[:, None, None] * point_strain / jnp.sqrt(1.0 + softening[:, None, None] * point_strain * point_strain)

def micro_model(strain_in, modal_state, localization, modes, scaled, point_modulus, softening, inverse):
    imposed = jnp.einsum('pj,jgz->pgz', localization, strain_in, precision=highest)
    for newton_step in range(ITERS):
        point_strain = imposed + jnp.einsum('pm,mgz->pgz', modes, modal_state, precision=highest)
        response = respond(point_strain, point_modulus, softening)
        residual = jnp.einsum('pm,pgz->mgz', modes, scaled[:, None, None] * response, precision=highest)
        modal_state = modal_state - jnp.einsum('mn,ngz->mgz', inverse, residual, precision=highest)
    point_strain = imposed + jnp.einsum('pm,mgz->pgz', modes, modal_state, precision=highest)
    response = respond(point_strain, point_modulus, softening)
    stress = jnp.einsum('pj,pgz->jgz', localization, scaled[:, None, None] * response, precision=highest)
    return (stress, modal_state)

def reference(displacement, velocity, external_force, node_mass, stiffness, cloak_list, micro_state, localization, modes, point_weight, point_modulus, softening):
    padded = jnp.pad(displacement, ((0, 0), (0, 1), (0, 1), (0, 1)))
    strain = voigt_strain(padded)
    stress = linear_stress(strain, stiffness)
    inverse = tangent_inverse(modes, point_weight, point_modulus)
    scaled = point_weight / localization.shape[0]
    strain_flat = strain.reshape(6, NX * NY, LZ)
    tile_count = N_GX * N_GY
    tile_lists = cloak_list.reshape(tile_count, CMAX)
    tile_states = micro_state.reshape(tile_count, M, CMAX, LZ)
    tile_number = jnp.arange(tile_count, dtype=jnp.int32)

    def per_tile(inputs):
        entries, modal_state, number = inputs
        listed = entries >= 0
        in_tile = jnp.maximum(entries, 0)
        global_x = number // N_GY * CX + in_tile // CY
        global_y = number % N_GY * CY + in_tile % CY
        pencil = (global_x * NY + global_y).astype(jnp.int32)
        tile_strain = jnp.take(strain_flat, pencil, axis=1)
        tile_stress, new_state = micro_model(tile_strain, modal_state, localization, modes, scaled, point_modulus, softening, inverse)
        new_state = jnp.where(listed[None, :, None], new_state, 0.0)
        target = jnp.where(listed, pencil, NX * NY).astype(jnp.int32)
        return (tile_stress, new_state, target)
    stresses, states, targets = lax.map(per_tile, (tile_lists, tile_states, tile_number))
    values = jnp.transpose(stresses, (1, 0, 2, 3)).reshape(6, tile_count * CMAX, LZ)
    stress = stress.reshape(6, NX * NY, LZ).at[:, targets.reshape(-1)].set(values, mode='drop')
    stress = stress.reshape(6, NX, NY, LZ)
    internal = assemble(stress, 1, 0)
    acceleration = (external_force - internal) / node_mass[None]
    velocity_next = velocity + step_size * acceleration
    displacement_next = displacement + step_size * velocity_next
    return (displacement_next, velocity_next, states.reshape(N_GX, N_GY, M, CMAX, LZ))
```

```python
import functools

import jax
import jax.numpy as jnp
from jax import lax
from jax.experimental import pallas as pl
from jax.experimental.pallas import tpu as pltpu
from jax.sharding import PartitionSpec as P

ITERS = 3
STEP = 0.25
F32 = jnp.float32
BF16 = jnp.bfloat16
MESH = pl.DeviceIdType.MESH
VMEM = pl.BlockSpec(memory_space=pltpu.VMEM)
SMEM = pl.BlockSpec(memory_space=pltpu.SMEM)
ANY = pl.BlockSpec(memory_space=pl.ANY)


def split(x):
    high = x.astype(BF16)
    low = (x - high.astype(F32)).astype(BF16)
    return high, low


def dot(a, b):
    return jnp.dot(a, b, preferred_element_type=F32)


def dot3(a, b):
    ah, al = split(a)
    bh, bl = split(b)
    return dot(jnp.concatenate([ah, ah, al], axis=1), jnp.concatenate([bh, bl, bh], axis=0))


def dot6(a, b):
    return jnp.dot(a, b, preferred_element_type=F32, precision=lax.Precision.HIGHEST)


def eye(n):
    rows = lax.broadcasted_iota(jnp.int32, (n, n), 0)
    columns = lax.broadcasted_iota(jnp.int32, (n, n), 1)
    return rows == columns


def total_square(x):
    return jnp.sum(jnp.sum(x * x, axis=0, keepdims=True), axis=1, keepdims=True)


def start_inverse(matrix, rounds):
    n = matrix.shape[0]
    diagonal = eye(n)
    unit = jnp.where(diagonal, 1.0, 0.0).astype(F32)
    inv_row = lax.rsqrt(jnp.sum(jnp.where(diagonal, matrix, 0.0), axis=0, keepdims=True))
    inv_column = lax.rsqrt(jnp.sum(jnp.where(diagonal, matrix, 0.0), axis=1, keepdims=True))
    scaled = matrix * inv_row * inv_column
    square = dot3(scaled, scaled)
    bound = jnp.max(jnp.sum(jnp.abs(square), axis=0, keepdims=True), axis=1, keepdims=True)
    c = 1.9 * lax.rsqrt(bound)
    x = (2.0 * c) * unit - (c * c) * scaled
    rest = unit - (2.0 * c) * scaled + (c * c) * square
    for _ in range(rounds):
        x = x + dot3(x, rest)
        rest = unit - dot3(scaled, x)
    return scaled, inv_column, x, rest


def finish_inverse(scaled, x, error):
    unit = jnp.where(eye(x.shape[0]), 1.0, 0.0).astype(F32)

    def unfinished(carry):
        count, error, _ = carry
        return jnp.logical_and(error > 1e-3, count < 40)

    def improve(carry):
        count, _, x = carry
        x = x + dot3(x, unit - dot3(scaled, x))
        rest = unit - dot3(scaled, x)
        return count + 1, jnp.sum(rest * rest), x

    _, _, x = lax.while_loop(unfinished, improve, (0, error, x))
    for _ in range(2):
        x = x + dot6(x, unit - dot6(scaled, x))
    return x


def neighbours():
    n_gx, n_gy = lax.axis_size("gx"), lax.axis_size("gy")
    gx, gy = lax.axis_index("gx"), lax.axis_index("gy")
    up = (lax.rem(gx + 1, n_gx), lax.rem(gy + 1, n_gy))
    down = (lax.rem(gx + n_gx - 1, n_gx), lax.rem(gy + n_gy - 1, n_gy))
    senders = [(up[0], gy), (gx, up[1]), up]
    targets = [(down[0], gy), (gx, down[1]), down]
    return senders, targets


def meet(others):
    barrier = pltpu.get_barrier_semaphore()
    for device in others:
        pl.semaphore_signal(barrier, inc=1, device_id=device, device_id_type=MESH)
    return barrier


def prepare_kernel(disp, modes_ref, loc_ref, weight_ref, modulus_ref, soft_ref,
                   w_ref, t_ref, scaled_ref, x_ref, column_ref, error_ref, project_ref, hx_ref, hy_ref, hc_ref,
                   loc_pad, rx, ry, rc, send_sem, recv_sem):
    uppers, lowers = neighbours()
    barrier = meet(uppers + lowers)
    loc_pad[...] = jnp.zeros_like(loc_pad)
    loc_pad[0:6, :] = loc_ref[...]
    pl.semaphore_wait(barrier, 6)
    copies = []
    for slot, (source, target, device) in enumerate([
        (disp.at[:, 0], rx, lowers[0]),
        (disp.at[:, :, 0:1], ry, lowers[1]),
        (disp.at[:, 0, 0:1], rc, lowers[2]),
    ]):
        copy = pltpu.make_async_remote_copy(
            src_ref=source, dst_ref=target, send_sem=send_sem.at[slot], recv_sem=recv_sem.at[slot],
            device_id=device, device_id_type=MESH)
        copy.start()
        copies.append(copy)

    points, m = modes_ref.shape
    modes = modes_ref[...]
    modes_t = modes.T
    loc_t = loc_pad[...]
    soft = soft_ref[...]
    inv_root = lax.rsqrt(soft)
    root = soft * inv_root
    weights = weight_ref[...] * modulus_ref[...] * (1.0 / points)
    scaled, inv_column, x, rest = start_inverse(dot6(modes_t * weights, modes), 6)
    scaled_ref[...] = scaled
    x_ref[...] = x
    column_ref[...] = -inv_column
    error_ref[...] = jnp.broadcast_to(total_square(rest), error_ref.shape)
    project_ref[...] = modes_t * (weights * inv_root) * inv_column
    t = jnp.concatenate([loc_t * (weights * inv_root), jnp.zeros((8, points), F32)], axis=0)
    th, tl = split(t)
    t_ref[...] = jnp.concatenate([th, th, tl], axis=1)
    mh, ml = split((modes_t * root).T)
    w_ref[:, 0:m] = mh
    w_ref[:, m : 2 * m] = mh
    w_ref[:, 2 * m : 3 * m] = ml
    lh = (loc_t * root).astype(BF16).astype(F32)
    ll = loc_t * root - lh
    local = jnp.concatenate([lh, lh, ll, jnp.zeros((m - 24, points), F32)], axis=0)
    w_ref[:, 3 * m : 4 * m] = local.T.astype(BF16)

    for copy in copies:
        copy.wait()
    last_x = lax.axis_index("gx") == lax.axis_size("gx") - 1
    last_y = lax.axis_index("gy") == lax.axis_size("gy") - 1
    keep_x = jnp.where(last_x, 0.0, 1.0)
    keep_y = jnp.where(last_y, 0.0, 1.0)
    hx_ref[...] = rx[...] * keep_x
    for row in range(hy_ref.shape[1]):
        hy_ref[:, row : row + 1, :] = ry[:, row] * keep_y
    hc_ref[...] = rc[...] * (keep_x * keep_y)


def prepare(disp, modes, loc, weight, modulus, soft):
    points, m = modes.shape
    rows, cols, layers = disp.shape[1:]
    row = lambda x: x.reshape(1, points)
    return pl.pallas_call(
        prepare_kernel,
        out_shape=(
            jax.ShapeDtypeStruct((points, 4 * m), BF16),
            jax.ShapeDtypeStruct((16, 3 * points), BF16),
            jax.ShapeDtypeStruct((m, m), F32),
            jax.ShapeDtypeStruct((m, m), F32),
            jax.ShapeDtypeStruct((m, 1), F32),
            jax.ShapeDtypeStruct((8, 128), F32),
            jax.ShapeDtypeStruct((m, points), F32),
            jax.ShapeDtypeStruct((3, cols, layers), F32),
            jax.ShapeDtypeStruct((3, rows, layers), F32),
            jax.ShapeDtypeStruct((3, 1, layers), F32),
        ),
        in_specs=[ANY] + [VMEM] * 5,
        out_specs=(VMEM,) * 10,
        scratch_shapes=[
            pltpu.VMEM((8, points), F32),
            pltpu.VMEM((3, cols, layers), F32),
            pltpu.VMEM((3, rows, 1, layers), F32),
            pltpu.VMEM((3, 1, layers), F32),
            pltpu.SemaphoreType.DMA((3,)),
            pltpu.SemaphoreType.DMA((3,)),
        ],
        compiler_params=pltpu.CompilerParams(collective_id=0, has_side_effects=True),
        name="prepare",
    )(disp, modes, loc.T, row(weight), row(modulus), row(soft))


def micro_kernel(list_ref, w_ref, t_ref, scaled_ref, x_ref, column_ref, error_ref, project_ref, hx_ref, hy_ref, hc_ref, disp_ref, stiff_ref, state_hbm,
                 new_hbm, force_ref, ex_ref, ey_ref, ec_ref,
                 g_ref, state, strain, stress, in_sem, out_sem):
    rows, cols, layers = stiff_ref.shape
    blocks = state.shape[0]
    m = state.shape[1] // 8
    points = w_ref.shape[0]
    member = lax.axis_index("gy")

    def fetch(b):
        return pltpu.make_async_copy(
            state_hbm.at[:, pl.ds(b * 8, 8), :], state.at[b].reshape(m, 8, layers), in_sem.at[b])

    def drain(b):
        return pltpu.make_async_copy(
            state.at[b].reshape(m, 8, layers), new_hbm.at[:, pl.ds(b * 8, 8), :], out_sem.at[b])

    for b in range(blocks):
        fetch(b).start()

    inverse = finish_inverse(scaled_ref[...], x_ref[...], error_ref[0, 0])
    gh, gl = split(column_ref[...] * dot6(inverse, project_ref[...]))
    g_ref[...] = jnp.concatenate([gh, gh, gl], axis=1)

    lane = lax.broadcasted_iota(jnp.int32, (cols, layers), 1)
    sub = lax.broadcasted_iota(jnp.int32, (cols, layers), 0)
    last_lane = lane == layers - 1
    first_lane = lane == 0
    last_sub = sub == cols - 1
    first_sub = sub == 0

    def node_terms(values, beyond):
        out = []
        for c in range(3):
            here = values[c]
            there = jnp.where(last_sub, beyond[c], pltpu.roll(here, cols - 1, 0))
            total = here + there
            slope = there - here
            above = jnp.where(last_lane, 0.0, pltpu.roll(total, layers - 1, 1))
            slope_above = jnp.where(last_lane, 0.0, pltpu.roll(slope, layers - 1, 1))
            out.append((total + above, slope + slope_above, above - total))
        return out

    def element_row(x, low, high):
        first = [0.25 * (high[c][0] - low[c][0]) for c in range(3)]
        second = [0.25 * (high[c][1] + low[c][1]) for c in range(3)]
        third = [0.25 * (high[c][2] + low[c][2]) for c in range(3)]
        e = [first[0], second[1], third[2], third[1] + second[2], third[0] + first[2], second[0] + first[1]]
        stiff = stiff_ref[x]
        volume = e[0] + e[1] + e[2]
        s = [stiff * (volume + 2.0 * e[c]) for c in range(3)] + [stiff * e[c] for c in range(3, 6)]
        for c in range(6):
            place = pl.ds(x * cols * 8 + c, cols, stride=8)
            strain[place, :] = e[c]
            stress[place, :] = s[c]
        for c in (6, 7):
            strain[pl.ds(x * cols * 8 + c, cols, stride=8), :] = jnp.zeros((cols, layers), F32)

    terms = node_terms([disp_ref[c, 0] for c in range(3)], [hy_ref[c, 0:1, :] for c in range(3)])
    for x in range(rows):
        if x + 1 < rows:
            later = node_terms([disp_ref[c, x + 1] for c in range(3)], [hy_ref[c, x + 1 : x + 2, :] for c in range(3)])
        else:
            later = node_terms([hx_ref[c] for c in range(3)], [hc_ref[c] for c in range(3)])
        element_row(x, terms, later)
        terms = later
    dummy = rows * cols
    strain[pl.ds(dummy * 8, 8), :] = jnp.zeros((8, layers), F32)

    def place_of(e):
        entry = list_ref[0, member, e]
        return entry >= 0, pl.multiple_of(jnp.where(entry >= 0, entry, dummy) * 8, 8)

    def sub_chunk(b, j):
        pair = [place_of(b * 8 + j + i) for i in range(2)]
        a = jnp.concatenate([state[b, pl.ds(j + i, m, stride=8), :] for i in range(2)], axis=1)
        e = jnp.concatenate([strain[pl.ds(pair[i][1], 8), :] for i in range(2)], axis=1)
        return pair, a, e

    def solve(chunks):
        u, a = [], []
        for _, amp, e in chunks:
            ah, al = split(amp)
            eh = e.astype(BF16).astype(F32)
            tail = jnp.concatenate([eh, e - eh], axis=0).astype(BF16)
            head = jnp.concatenate([eh, jnp.zeros_like(eh)], axis=0).astype(BF16)
            rhs = jnp.concatenate([ah, al, ah, tail, head], axis=0)
            u.append(dot(w_ref[:, 0 : 3 * m + 32], rhs))
            a.append(amp)
        count = len(chunks)
        for _ in range(ITERS):
            deltas = []
            for c in range(count):
                rh, rl = split(u[c] * lax.rsqrt(1.0 + u[c] * u[c]))
                deltas.append(dot(g_ref[...], jnp.concatenate([rh, rl, rh], axis=0)))
            for c in range(count):
                dh, dl = split(deltas[c])
                a[c] = a[c] + deltas[c]
                u[c] = u[c] + dot(w_ref[:, 0 : 3 * m], jnp.concatenate([dh, dl, dh], axis=0))
        out = []
        for c in range(count):
            rh, rl = split(u[c] * lax.rsqrt(1.0 + u[c] * u[c]))
            out.append(dot(t_ref[...], jnp.concatenate([rh, rl, rh], axis=0)))
        return a, out

    total = jnp.int32(0)
    for e in range(blocks * 8):
        total = total + jnp.where(list_ref[0, member, e] >= 0, 1, 0)

    def block_step(b, carry):
        fetch(b).wait()
        for half in range(2):
            base = b * 8 + half * 4

            @pl.when(base < total)
            def _():
                chunks = [sub_chunk(b, half * 4 + 2 * c) for c in range(2)]
                a, out = solve(chunks)
                for c in range(2):
                    for i in range(2):
                        listed, place = chunks[c][0][i]
                        columns = slice(i * layers, (i + 1) * layers)
                        keep = jnp.where(listed, 1.0, 0.0)
                        state[b, pl.ds(half * 4 + 2 * c + i, m, stride=8), :] = a[c][:, columns] * keep
                        stress[pl.ds(place, 8), :] = out[c][0:8, columns]

            @pl.when(base >= total)
            def _():
                for i in range(4):
                    state[b, pl.ds(half * 4 + i, m, stride=8), :] = jnp.zeros((m, layers), F32)

        drain(b).start()
        return carry

    lax.fori_loop(0, blocks, block_step, 0)

    def element_terms(x):
        s = [stress[pl.ds(x * cols * 8 + c, cols, stride=8), :] for c in range(6)]
        below = [jnp.where(first_lane, 0.0, pltpu.roll(s[c], 1, 1)) for c in range(6)]
        zsum = [s[c] + below[c] for c in range(6)]
        zdiff = [s[c] - below[c] for c in range(6)]
        p = [zsum[0], zsum[5], zsum[4]]
        q = [zsum[5], zsum[1], zsum[3]]
        r = [zdiff[4], zdiff[3], zdiff[2]]
        out = []
        for i in range(3):
            plus, minus = r[i] + q[i], r[i] - q[i]
            out.append((plus + p[i], plus - p[i], minus + p[i], minus - p[i]))
        return out

    def node_row(own, above):
        rolled = pltpu.roll(above, 1, 0)
        return -0.25 * (own + jnp.where(first_sub, 0.0, rolled)), -0.25 * rolled[0:1, :]

    zero = jnp.zeros((cols, layers), F32)
    before = [(zero, zero)] * 3
    for x in range(rows):
        terms = element_terms(x)
        for i in range(3):
            inner, edge = node_row(terms[i][0] + before[i][0], terms[i][2] + before[i][1])
            force_ref[i, x] = inner
            ey_ref[i, x : x + 1, :] = edge
        before = [(terms[i][1], terms[i][3]) for i in range(3)]
    for i in range(3):
        inner, edge = node_row(before[i][0], before[i][1])
        ex_ref[i] = inner
        ec_ref[i] = edge
    for b in range(blocks):
        drain(b).wait()


def micro(cloak_list, constants, halos, disp, stiff, state):
    m, slots, layers = state.shape
    rows, cols, _ = stiff.shape
    blocks = slots // 8
    return pl.pallas_call(
        micro_kernel,
        out_shape=(
            jax.ShapeDtypeStruct(state.shape, F32),
            jax.ShapeDtypeStruct((3, rows, cols, layers), F32),
            jax.ShapeDtypeStruct((3, cols, layers), F32),
            jax.ShapeDtypeStruct((3, rows, layers), F32),
            jax.ShapeDtypeStruct((3, 1, layers), F32),
        ),
        in_specs=[SMEM] + [VMEM] * 12 + [ANY],
        out_specs=(ANY, VMEM, VMEM, VMEM, VMEM),
        scratch_shapes=[
            pltpu.VMEM((m, constants[1].shape[1]), BF16),
            pltpu.VMEM((blocks, m * 8, layers), F32),
            pltpu.VMEM(((rows * cols + 1) * 8, layers), F32),
            pltpu.VMEM(((rows * cols + 1) * 8, layers), F32),
            pltpu.SemaphoreType.DMA((blocks,)),
            pltpu.SemaphoreType.DMA((blocks,)),
        ],
        name="micro",
    )(cloak_list, *constants, *halos, disp, stiff, state)


def join_kernel(force_ref, ex_ref, ey_ref, ec_ref, out_ref, rx, ry, rc, send_sem, recv_sem):
    uppers, lowers = neighbours()
    barrier = meet(uppers + lowers)
    pl.semaphore_wait(barrier, 6)
    copies = []
    for slot, (source, target, device) in enumerate([
        (ex_ref, rx, uppers[0]), (ey_ref, ry, uppers[1]), (ec_ref, rc, uppers[2]),
    ]):
        copy = pltpu.make_async_remote_copy(
            src_ref=source, dst_ref=target, send_sem=send_sem.at[slot], recv_sem=recv_sem.at[slot],
            device_id=device, device_id_type=MESH)
        copy.start()
        copies.append(copy)
    out_ref[...] = force_ref[...]
    for copy in copies:
        copy.wait()
    keep_x = jnp.where(lax.axis_index("gx") == 0, 0.0, 1.0)
    keep_y = jnp.where(lax.axis_index("gy") == 0, 0.0, 1.0)
    out_ref[:, 0] = out_ref[:, 0] + rx[...] * keep_x
    for i in range(3):
        out_ref[i, :, 0, :] = out_ref[i, :, 0, :] + ry[i] * keep_y
        out_ref[i, 0, 0:1, :] = out_ref[i, 0, 0:1, :] + rc[i] * (keep_x * keep_y)


def join(force, ex, ey, ec):
    return pl.pallas_call(
        join_kernel,
        out_shape=jax.ShapeDtypeStruct(force.shape, F32),
        in_specs=[VMEM] * 4,
        out_specs=VMEM,
        scratch_shapes=[
            pltpu.VMEM(ex.shape, F32),
            pltpu.VMEM(ey.shape, F32),
            pltpu.VMEM(ec.shape, F32),
            pltpu.SemaphoreType.DMA((3,)),
            pltpu.SemaphoreType.DMA((3,)),
        ],
        compiler_params=pltpu.CompilerParams(collective_id=1, has_side_effects=True),
        name="join",
    )(force, ex, ey, ec)


def on_device(displacement, velocity, external_force, node_mass, stiffness, cloak_list, micro_state,
              localization, modes, point_weight, point_modulus, softening):
    prepared = prepare(displacement, modes, localization, point_weight, point_modulus, softening)
    new_state, force, ex, ey, ec = micro(
        cloak_list, prepared[:7], prepared[7:], displacement, stiffness, micro_state[0, 0])
    internal = join(force, ex, ey, ec)
    velocity_next = velocity + STEP * (external_force - internal) / node_mass[None]
    displacement_next = displacement + STEP * velocity_next
    return displacement_next, velocity_next, new_state[None, None]


def solution(mesh):
    grid = P(None, "gx", "gy", None)
    tile = P("gx", "gy", None)
    state = P("gx", "gy", None, None, None)
    return jax.shard_map(
        on_device,
        mesh=mesh,
        in_specs=(grid, grid, grid, tile, tile, P("gx", None, None), state, P(), P(), P(), P(), P()),
        out_specs=(grid, grid, state),
        check_vma=False,
    )
```

```python
import functools

import jax
import jax.numpy as jnp
from jax import lax
from jax.experimental import pallas as pl
from jax.experimental.pallas import tpu as pltpu
from jax.sharding import PartitionSpec as P

ITERS = 3
STEP = 0.25
F32 = jnp.float32
BF16 = jnp.bfloat16
MESH = pl.DeviceIdType.MESH
VMEM = pl.BlockSpec(memory_space=pltpu.VMEM)
SMEM = pl.BlockSpec(memory_space=pltpu.SMEM)
ANY = pl.BlockSpec(memory_space=pl.ANY)


def split(x):
    high = x.astype(BF16)
    low = (x - high.astype(F32)).astype(BF16)
    return high, low


def dot(a, b):
    return jnp.dot(a, b, preferred_element_type=F32)


def dot3(a, b):
    ah, al = split(a)
    bh, bl = split(b)
    return dot(jnp.concatenate([ah, ah, al], axis=1), jnp.concatenate([bh, bl, bh], axis=0))


def dot6(a, b):
    return jnp.dot(a, b, preferred_element_type=F32, precision=lax.Precision.HIGHEST)


def eye(n):
    rows = lax.broadcasted_iota(jnp.int32, (n, n), 0)
    columns = lax.broadcasted_iota(jnp.int32, (n, n), 1)
    return rows == columns


def total_square(x):
    return jnp.sum(jnp.sum(x * x, axis=0, keepdims=True), axis=1, keepdims=True)


def start_inverse(matrix, rounds):
    n = matrix.shape[0]
    diagonal = eye(n)
    unit = jnp.where(diagonal, 1.0, 0.0).astype(F32)
    inv_row = lax.rsqrt(jnp.sum(jnp.where(diagonal, matrix, 0.0), axis=0, keepdims=True))
    inv_column = lax.rsqrt(jnp.sum(jnp.where(diagonal, matrix, 0.0), axis=1, keepdims=True))
    scaled = matrix * inv_row * inv_column
    square = dot3(scaled, scaled)
    bound = jnp.max(jnp.sum(jnp.abs(square), axis=0, keepdims=True), axis=1, keepdims=True)
    c = 1.9 * lax.rsqrt(bound)
    x = (2.0 * c) * unit - (c * c) * scaled
    rest = unit - (2.0 * c) * scaled + (c * c) * square
    for _ in range(rounds):
        x = x + dot3(x, rest)
        rest = unit - dot3(scaled, x)
    return scaled, inv_column, x, rest


def finish_inverse(scaled, x, error):
    unit = jnp.where(eye(x.shape[0]), 1.0, 0.0).astype(F32)

    def unfinished(carry):
        count, error, _ = carry
        return jnp.logical_and(error > 1e-3, count < 40)

    def improve(carry):
        count, _, x = carry
        x = x + dot3(x, unit - dot3(scaled, x))
        rest = unit - dot3(scaled, x)
        return count + 1, jnp.sum(rest * rest), x

    _, _, x = lax.while_loop(unfinished, improve, (0, error, x))
    for _ in range(2):
        x = x + dot6(x, unit - dot6(scaled, x))
    return x


def neighbours():
    n_gx, n_gy = lax.axis_size("gx"), lax.axis_size("gy")
    gx, gy = lax.axis_index("gx"), lax.axis_index("gy")
    up = (lax.rem(gx + 1, n_gx), lax.rem(gy + 1, n_gy))
    down = (lax.rem(gx + n_gx - 1, n_gx), lax.rem(gy + n_gy - 1, n_gy))
    senders = [(up[0], gy), (gx, up[1]), up]
    targets = [(down[0], gy), (gx, down[1]), down]
    return senders, targets


def meet(others):
    barrier = pltpu.get_barrier_semaphore()
    for device in others:
        pl.semaphore_signal(barrier, inc=1, device_id=device, device_id_type=MESH)
    return barrier


def prepare_kernel(disp, modes_ref, loc_ref, weight_ref, modulus_ref, soft_ref,
                   w_ref, t_ref, scaled_ref, x_ref, column_ref, error_ref, project_ref, hx_ref, hy_ref, hc_ref,
                   loc_pad, rx, ry, rc, send_sem, recv_sem):
    uppers, lowers = neighbours()
    barrier = meet(uppers + lowers)
    loc_pad[...] = jnp.zeros_like(loc_pad)
    loc_pad[0:6, :] = loc_ref[...]
    pl.semaphore_wait(barrier, 6)
    copies = []
    for slot, (source, target, device) in enumerate([
        (disp.at[:, 0], rx, lowers[0]),
        (disp.at[:, :, 0:1], ry, lowers[1]),
        (disp.at[:, 0, 0:1], rc, lowers[2]),
    ]):
        copy = pltpu.make_async_remote_copy(
            src_ref=source, dst_ref=target, send_sem=send_sem.at[slot], recv_sem=recv_sem.at[slot],
            device_id=device, device_id_type=MESH)
        copy.start()
        copies.append(copy)

    points, m = modes_ref.shape
    modes = modes_ref[...]
    modes_t = modes.T
    loc_t = loc_pad[...]
    soft = soft_ref[...]
    inv_root = lax.rsqrt(soft)
    root = soft * inv_root
    weights = weight_ref[...] * modulus_ref[...] * (1.0 / points)
    scaled, inv_column, x, rest = start_inverse(dot6(modes_t * weights, modes), 6)
    scaled_ref[...] = scaled
    x_ref[...] = x
    column_ref[...] = -inv_column
    error_ref[...] = jnp.broadcast_to(total_square(rest), error_ref.shape)
    project_ref[...] = modes_t * (weights * inv_root) * inv_column
    t = jnp.concatenate([loc_t * (weights * inv_root), jnp.zeros((8, points), F32)], axis=0)
    th, tl = split(t)
    t_ref[...] = jnp.concatenate([th, th, tl], axis=1)
    mh, ml = split((modes_t * root).T)
    w_ref[:, 0:m] = mh
    w_ref[:, m : 2 * m] = mh
    w_ref[:, 2 * m : 3 * m] = ml
    lh = (loc_t * root).astype(BF16).astype(F32)
    ll = loc_t * root - lh
    local = jnp.concatenate([lh, lh, ll, jnp.zeros((m - 24, points), F32)], axis=0)
    w_ref[:, 3 * m : 4 * m] = local.T.astype(BF16)

    for copy in copies:
        copy.wait()
    last_x = lax.axis_index("gx") == lax.axis_size("gx") - 1
    last_y = lax.axis_index("gy") == lax.axis_size("gy") - 1
    keep_x = jnp.where(last_x, 0.0, 1.0)
    keep_y = jnp.where(last_y, 0.0, 1.0)
    hx_ref[...] = rx[...] * keep_x
    for row in range(hy_ref.shape[1]):
        hy_ref[:, row : row + 1, :] = ry[:, row] * keep_y
    hc_ref[...] = rc[...] * (keep_x * keep_y)


def prepare(disp, modes, loc, weight, modulus, soft):
    points, m = modes.shape
    rows, cols, layers = disp.shape[1:]
    row = lambda x: x.reshape(1, points)
    return pl.pallas_call(
        prepare_kernel,
        out_shape=(
            jax.ShapeDtypeStruct((points, 4 * m), BF16),
            jax.ShapeDtypeStruct((16, 3 * points), BF16),
            jax.ShapeDtypeStruct((m, m), F32),
            jax.ShapeDtypeStruct((m, m), F32),
            jax.ShapeDtypeStruct((m, 1), F32),
            jax.ShapeDtypeStruct((8, 128), F32),
            jax.ShapeDtypeStruct((m, points), F32),
            jax.ShapeDtypeStruct((3, cols, layers), F32),
            jax.ShapeDtypeStruct((3, rows, layers), F32),
            jax.ShapeDtypeStruct((3, 1, layers), F32),
        ),
        in_specs=[ANY] + [VMEM] * 5,
        out_specs=(VMEM,) * 10,
        scratch_shapes=[
            pltpu.VMEM((8, points), F32),
            pltpu.VMEM((3, cols, layers), F32),
            pltpu.VMEM((3, rows, 1, layers), F32),
            pltpu.VMEM((3, 1, layers), F32),
            pltpu.SemaphoreType.DMA((3,)),
            pltpu.SemaphoreType.DMA((3,)),
        ],
        compiler_params=pltpu.CompilerParams(collective_id=0, has_side_effects=True),
        name="prepare",
    )(disp, modes, loc.T, row(weight), row(modulus), row(soft))


def micro_kernel(list_ref, w_ref, t_ref, scaled_ref, x_ref, column_ref, error_ref, project_ref, hx_ref, hy_ref, hc_ref, disp_ref, stiff_ref, state_hbm,
                 new_hbm, force_ref, ex_ref, ey_ref, ec_ref,
                 g_ref, h_ref, state, strain, stress, in_sem, out_sem):
    rows, cols, layers = stiff_ref.shape
    blocks = state.shape[0]
    m = state.shape[1] // 8
    points = w_ref.shape[0]
    member = lax.axis_index("gy")

    def fetch(b):
        return pltpu.make_async_copy(
            state_hbm.at[:, pl.ds(b * 8, 8), :], state.at[b].reshape(m, 8, layers), in_sem.at[b])

    def drain(b):
        return pltpu.make_async_copy(
            state.at[b].reshape(m, 8, layers), new_hbm.at[:, pl.ds(b * 8, 8), :], out_sem.at[b])

    for b in range(blocks):
        fetch(b).start()

    inverse = finish_inverse(scaled_ref[...], x_ref[...], error_ref[0, 0])
    gh, gl = split(column_ref[...] * dot6(inverse, project_ref[...]))
    g_ref[...] = jnp.concatenate([gh, gh, gl], axis=1)
    hh, hl = split(dot(w_ref[:, 0 : 3 * m], jnp.concatenate([gh, gl, gh], axis=0)))
    h_ref[...] = jnp.concatenate([hh, hh, hl], axis=1)

    lane = lax.broadcasted_iota(jnp.int32, (cols, layers), 1)
    sub = lax.broadcasted_iota(jnp.int32, (cols, layers), 0)
    last_lane = lane == layers - 1
    first_lane = lane == 0
    last_sub = sub == cols - 1
    first_sub = sub == 0

    def node_terms(values, beyond):
        out = []
        for c in range(3):
            here = values[c]
            there = jnp.where(last_sub, beyond[c], pltpu.roll(here, cols - 1, 0))
            total = here + there
            slope = there - here
            above = jnp.where(last_lane, 0.0, pltpu.roll(total, layers - 1, 1))
            slope_above = jnp.where(last_lane, 0.0, pltpu.roll(slope, layers - 1, 1))
            out.append((total + above, slope + slope_above, above - total))
        return out

    def element_row(x, low, high):
        first = [0.25 * (high[c][0] - low[c][0]) for c in range(3)]
        second = [0.25 * (high[c][1] + low[c][1]) for c in range(3)]
        third = [0.25 * (high[c][2] + low[c][2]) for c in range(3)]
        e = [first[0], second[1], third[2], third[1] + second[2], third[0] + first[2], second[0] + first[1]]
        stiff = stiff_ref[x]
        volume = e[0] + e[1] + e[2]
        s = [stiff * (volume + 2.0 * e[c]) for c in range(3)] + [stiff * e[c] for c in range(3, 6)]
        for c in range(6):
            place = pl.ds(x * cols * 8 + c, cols, stride=8)
            strain[place, :] = e[c]
            stress[place, :] = s[c]
        for c in (6, 7):
            strain[pl.ds(x * cols * 8 + c, cols, stride=8), :] = jnp.zeros((cols, layers), F32)

    terms = node_terms([disp_ref[c, 0] for c in range(3)], [hy_ref[c, 0:1, :] for c in range(3)])
    for x in range(rows):
        if x + 1 < rows:
            later = node_terms([disp_ref[c, x + 1] for c in range(3)], [hy_ref[c, x + 1 : x + 2, :] for c in range(3)])
        else:
            later = node_terms([hx_ref[c] for c in range(3)], [hc_ref[c] for c in range(3)])
        element_row(x, terms, later)
        terms = later
    dummy = rows * cols
    strain[pl.ds(dummy * 8, 8), :] = jnp.zeros((8, layers), F32)

    def place_of(e):
        entry = list_ref[0, member, e]
        return entry >= 0, pl.multiple_of(jnp.where(entry >= 0, entry, dummy) * 8, 8)

    def sub_chunk(b, j):
        pair = [place_of(b * 8 + j + i) for i in range(2)]
        a = jnp.concatenate([state[b, pl.ds(j + i, m, stride=8), :] for i in range(2)], axis=1)
        e = jnp.concatenate([strain[pl.ds(pair[i][1], 8), :] for i in range(2)], axis=1)
        return pair, a, e

    def solve(chunks):
        u, sums = [], []
        for _, amp, e in chunks:
            ah, al = split(amp)
            eh = e.astype(BF16).astype(F32)
            tail = jnp.concatenate([eh, e - eh], axis=0).astype(BF16)
            head = jnp.concatenate([eh, jnp.zeros_like(eh)], axis=0).astype(BF16)
            u.append(dot(w_ref[:, 0 : 3 * m + 32], jnp.concatenate([ah, al, ah, tail, head], axis=0)))
        count = len(chunks)
        for step in range(ITERS):
            for c in range(count):
                r = u[c] * lax.rsqrt(1.0 + u[c] * u[c])
                if step < ITERS - 1:
                    rh, rl = split(r)
                    u[c] = u[c] + dot(h_ref[...], jnp.concatenate([rh, rl, rh], axis=0))
                else:
                    u[c] = u[c] + dot(h_ref[:, 0:points], r.astype(BF16))
                if step == 0:
                    sums.append(r)
                else:
                    sums[c] = sums[c] + r
        a, out = [], []
        for c in range(count):
            sh, sl = split(sums[c])
            a.append(chunks[c][1] + dot(g_ref[...], jnp.concatenate([sh, sl, sh], axis=0)))
        for c in range(count):
            rh, rl = split(u[c] * lax.rsqrt(1.0 + u[c] * u[c]))
            out.append(dot(t_ref[...], jnp.concatenate([rh, rl, rh], axis=0)))
        return a, out

    total = jnp.int32(0)
    for e in range(blocks * 8):
        total = total + jnp.where(list_ref[0, member, e] >= 0, 1, 0)

    def block_step(b, carry):
        fetch(b).wait()
        base = b * 8

        @pl.when(base < total)
        def _():
            chunks = [sub_chunk(b, 2 * c) for c in range(4)]
            a, out = solve(chunks)
            for c in range(4):
                for i in range(2):
                    listed, place = chunks[c][0][i]
                    columns = slice(i * layers, (i + 1) * layers)
                    keep = jnp.where(listed, 1.0, 0.0)
                    state[b, pl.ds(2 * c + i, m, stride=8), :] = a[c][:, columns] * keep
                    stress[pl.ds(place, 8), :] = out[c][0:8, columns]

        @pl.when(base >= total)
        def _():
            state[b] = jnp.zeros((m * 8, layers), F32)

        drain(b).start()
        return carry

    lax.fori_loop(0, blocks, block_step, 0)

    def element_terms(x):
        s = [stress[pl.ds(x * cols * 8 + c, cols, stride=8), :] for c in range(6)]
        below = [jnp.where(first_lane, 0.0, pltpu.roll(s[c], 1, 1)) for c in range(6)]
        zsum = [s[c] + below[c] for c in range(6)]
        zdiff = [s[c] - below[c] for c in range(6)]
        p = [zsum[0], zsum[5], zsum[4]]
        q = [zsum[5], zsum[1], zsum[3]]
        r = [zdiff[4], zdiff[3], zdiff[2]]
        out = []
        for i in range(3):
            plus, minus = r[i] + q[i], r[i] - q[i]
            out.append((plus + p[i], plus - p[i], minus + p[i], minus - p[i]))
        return out

    def node_row(own, above):
        rolled = pltpu.roll(above, 1, 0)
        return -0.25 * (own + jnp.where(first_sub, 0.0, rolled)), -0.25 * rolled[0:1, :]

    zero = jnp.zeros((cols, layers), F32)
    before = [(zero, zero)] * 3
    for x in range(rows):
        terms = element_terms(x)
        for i in range(3):
            inner, edge = node_row(terms[i][0] + before[i][0], terms[i][2] + before[i][1])
            force_ref[i, x] = inner
            ey_ref[i, x : x + 1, :] = edge
        before = [(terms[i][1], terms[i][3]) for i in range(3)]
    for i in range(3):
        inner, edge = node_row(before[i][0], before[i][1])
        ex_ref[i] = inner
        ec_ref[i] = edge
    for b in range(blocks):
        drain(b).wait()


def micro(cloak_list, constants, halos, disp, stiff, state):
    m, slots, layers = state.shape
    rows, cols, _ = stiff.shape
    blocks = slots // 8
    return pl.pallas_call(
        micro_kernel,
        out_shape=(
            jax.ShapeDtypeStruct(state.shape, F32),
            jax.ShapeDtypeStruct((3, rows, cols, layers), F32),
            jax.ShapeDtypeStruct((3, cols, layers), F32),
            jax.ShapeDtypeStruct((3, rows, layers), F32),
            jax.ShapeDtypeStruct((3, 1, layers), F32),
        ),
        in_specs=[SMEM] + [VMEM] * 12 + [ANY],
        out_specs=(ANY, VMEM, VMEM, VMEM, VMEM),
        scratch_shapes=[
            pltpu.VMEM((m, constants[1].shape[1]), BF16),
            pltpu.VMEM((constants[0].shape[0], constants[1].shape[1]), BF16),
            pltpu.VMEM((blocks, m * 8, layers), F32),
            pltpu.VMEM(((rows * cols + 1) * 8, layers), F32),
            pltpu.VMEM(((rows * cols + 1) * 8, layers), F32),
            pltpu.SemaphoreType.DMA((blocks,)),
            pltpu.SemaphoreType.DMA((blocks,)),
        ],
        name="micro",
    )(cloak_list, *constants, *halos, disp, stiff, state)


def join_kernel(force_ref, ex_ref, ey_ref, ec_ref, out_ref, rx, ry, rc, send_sem, recv_sem):
    uppers, lowers = neighbours()
    barrier = meet(uppers + lowers)
    pl.semaphore_wait(barrier, 6)
    copies = []
    for slot, (source, target, device) in enumerate([
        (ex_ref, rx, uppers[0]), (ey_ref, ry, uppers[1]), (ec_ref, rc, uppers[2]),
    ]):
        copy = pltpu.make_async_remote_copy(
            src_ref=source, dst_ref=target, send_sem=send_sem.at[slot], recv_sem=recv_sem.at[slot],
            device_id=device, device_id_type=MESH)
        copy.start()
        copies.append(copy)
    out_ref[...] = force_ref[...]
    for copy in copies:
        copy.wait()
    keep_x = jnp.where(lax.axis_index("gx") == 0, 0.0, 1.0)
    keep_y = jnp.where(lax.axis_index("gy") == 0, 0.0, 1.0)
    out_ref[:, 0] = out_ref[:, 0] + rx[...] * keep_x
    for i in range(3):
        out_ref[i, :, 0, :] = out_ref[i, :, 0, :] + ry[i] * keep_y
        out_ref[i, 0, 0:1, :] = out_ref[i, 0, 0:1, :] + rc[i] * (keep_x * keep_y)


def join(force, ex, ey, ec):
    return pl.pallas_call(
        join_kernel,
        out_shape=jax.ShapeDtypeStruct(force.shape, F32),
        in_specs=[VMEM] * 4,
        out_specs=VMEM,
        scratch_shapes=[
            pltpu.VMEM(ex.shape, F32),
            pltpu.VMEM(ey.shape, F32),
            pltpu.VMEM(ec.shape, F32),
            pltpu.SemaphoreType.DMA((3,)),
            pltpu.SemaphoreType.DMA((3,)),
        ],
        compiler_params=pltpu.CompilerParams(collective_id=1, has_side_effects=True),
        name="join",
    )(force, ex, ey, ec)


def on_device(displacement, velocity, external_force, node_mass, stiffness, cloak_list, micro_state,
              localization, modes, point_weight, point_modulus, softening):
    prepared = prepare(displacement, modes, localization, point_weight, point_modulus, softening)
    new_state, force, ex, ey, ec = micro(
        cloak_list, prepared[:7], prepared[7:], displacement, stiffness, micro_state[0, 0])
    internal = join(force, ex, ey, ec)
    velocity_next = velocity + STEP * (external_force - internal) / node_mass[None]
    displacement_next = displacement + STEP * velocity_next
    return displacement_next, velocity_next, new_state[None, None]


def solution(mesh):
    grid = P(None, "gx", "gy", None)
    tile = P("gx", "gy", None)
    state = P("gx", "gy", None, None, None)
    return jax.shard_map(
        on_device,
        mesh=mesh,
        in_specs=(grid, grid, grid, tile, tile, P("gx", None, None), state, P(), P(), P(), P(), P()),
        out_specs=(grid, grid, state),
        check_vma=False,
    )
```
